32 devices in a mesh: groups: 2 (over x), grid: 16 (over z, y, core).
Axes of the slice: x: 2, y: 2, z: 4, core: 2. Of those that a mesh axis runs over, the one named last changes fastest.
Arguments:
- hist: float32 [768, 256, 256], P('groups', 'grid'), parts along dimension 0, may hold values from 0.2 to 2
- drift: float32 [2, 256, 256], P(None, 'grid'), may hold values from -0.5 to 0.5
- shocks: int32 [768, 2], P('groups'), parts along dimension 0, may hold values from 0 to 7
- shock_table: float32 [16, 2], P('groups'), parts along dimension 0, may hold values from -0.3 to 0.3
- first_weight: bfloat16 [131072, 2048], P(('groups', 'grid')), parts along dimension 0, may hold values from -0.03125 to 0.03125
- mid_weight: bfloat16 [4096, 2048], P('groups', 'grid'), parts along dimension 0, may hold values from -0.1875 to 0.1875
- head_weight: float32 [4096], P(('groups', 'grid')), parts along dimension 0, may hold values from -0.125 to 0.125
- cotangent: float32 [768], P('groups'), parts along dimension 0, may hold values from -6 to 6
Outputs:
- hist_next: float32 [768, 256, 256], P('groups', 'grid'), parts along dimension 0
- value: float32 [768], P('groups'), parts along dimension 0
- grad_first: bfloat16 [131072, 2048], P(('groups', 'grid')), parts along dimension 0
- grad_mid: bfloat16 [4096, 2048], P('groups', 'grid'), parts along dimension 0
- grad_head: float32 [4096], P(('groups', 'grid')), parts along dimension 0
The draws below stay inside these ranges and needn't reach their ends.
There are 2 independent parts, one for each index of `groups`. The reference program is written for one: setup_inputs(seed, part) draws one part's arguments, and reference() takes and returns one part's arrays. A program takes and returns all parts, laid end to end along the dimension named above; an argument that names none is the same for every part. Nothing has to cross between parts.
All inputs are finite; a program needn't handle non-finite values.
Results may differ from the reference program's by a relative error of at most 0.0173.
Values may be sent and summed in bfloat16 or wider, within the bound.
A program may use at most 128 MiB of HBM per device.

```python
import math
import jax
import jax.numpy as jnp
from jax import lax

G = 256
HID = 2048
S = 384
STEPS = 2
NSHOCK = 8
CELLS = 65536


def set_ends(result, key, low, high):
    longest = result.shape.index(max(result.shape))
    spots = []
    for shift in (0, 1):
        where = [jax.random.randint(jax.random.fold_in(key, axis), (), 0, length) for axis, length in enumerate(result.shape)]
        where[longest] = (where[longest] + shift) % result.shape[longest]
        spots.append(tuple(where))
    return result.at[spots[0]].set(low).at[spots[1]].set(high)


def raised(values, stream_key, source, target, parts, factor):
    owner, partner = [(jnp.arange(values.shape[dim]) // (values.shape[dim] // parts)).reshape([-1 if axis == dim else 1 for axis in range(values.ndim)]) for dim in (source, target)]
    chosen = jax.random.permutation(stream_key, parts)[partner]
    strong = (owner == chosen) | (owner == (partner + parts // 2) % parts)
    return jnp.where(strong, factor * values, values)


def levels(stream_key, extent, shards, smallest, top_value):
    factor_of = 1.0
    for axis_at, blocks in shards:
        heights = jax.random.uniform(jax.random.fold_in(jax.random.fold_in(stream_key, 6), axis_at), (blocks,), jnp.float32, smallest / len(shards), top_value / len(shards))
        factor_of = factor_of * jnp.repeat(jnp.exp(heights), extent[axis_at] // blocks).reshape((-1,) + (1,) * (len(extent) - 1 - axis_at))
    return factor_of


def bell_draw(key, extent, width, reach, shards=(), kind=jnp.bfloat16):
    drawn = width * jax.random.normal(key, extent, jnp.float32)
    if shards:
        drawn = drawn * levels(key, extent, shards, -0.22, 0.18)
    return jnp.clip(drawn, -reach, reach).astype(kind)


def bell_draw_with(own_key, shape, deviation, bound, shards, heavy, kind=jnp.bfloat16):
    drawn = deviation * jax.random.normal(own_key, shape, jnp.float32)
    if shards:
        drawn = drawn * levels(own_key, shape, shards, -0.22, 0.18)
    return jnp.clip(raised(drawn, jax.random.fold_in(own_key, 3), *heavy), -bound, bound).astype(kind)


def setup_inputs(seed: int = 0, part: int = 0) -> dict:
    key_of = jax.random.split(jax.random.key(seed), 9)
    own_keys = jax.random.split(jax.random.fold_in(key_of[8], part), 9)
    hist = jnp.clip(jnp.exp(math.log(2.0) - 2.3025851 * jax.random.uniform(own_keys[0], (S, G, G), jnp.float32) ** levels(own_keys[0], (S, G, G), ((1, 16),), -0.2, 0.2)), 0.2, 2.0)
    drift = jnp.clip(jax.random.uniform(key_of[1], (2, G, G), jnp.float32, -0.5, 0.5) * levels(key_of[1], (2, G, G), ((1, 16),), -0.4, 0.0), -0.5, 0.5)
    shocks = set_ends(jax.random.randint(own_keys[2], (S, STEPS), 0, NSHOCK), jax.random.fold_in(own_keys[2], 1), 0, NSHOCK - 1).astype(jnp.int32)
    shock_table = jnp.clip(jax.random.uniform(own_keys[3], (NSHOCK, 2), jnp.float32, -0.3, 0.3), -0.3, 0.3)
    first_weight = bell_draw_with(own_keys[4], (CELLS, HID), CELLS ** -0.5, 0.03125, ((0, 16),), (0, 1, 16, 2.0))
    mid_weight = bell_draw_with(own_keys[5], (HID, HID), HID ** -0.5, 0.1875, ((1, 16),), (1, 0, 16, 2.0))
    head_weight = bell_draw(own_keys[6], (HID,), HID ** -0.5, 0.125, ((0, 16),), jnp.float32)
    cotangent = bell_draw(own_keys[7], (S,), 1.0, 6.0, (), jnp.float32)
    return dict(hist=hist, drift=drift, shocks=shocks, shock_table=shock_table, first_weight=first_weight, mid_weight=mid_weight, head_weight=head_weight, cotangent=cotangent)


diffusion_rate = 0.24


def column_shift(values, offset):
    zero_col = jnp.zeros_like(values[..., :1])
    if offset > 0:
        return jnp.concatenate([values[..., 1:], zero_col], axis=-1)
    return jnp.concatenate([zero_col, values[..., :-1]], axis=-1)


def shock_shift(levels_now, table):
    level_ids = jnp.arange(table.shape[0], dtype=jnp.int32)
    onehot = (levels_now[:, None] == level_ids[None, :]).astype(jnp.float32)
    return jnp.sum(onehot[:, :, None] * table[None, :, :], axis=1)


def kfe_step(padded, drift_rows, shift_x, shift_y):
    velocity_x = drift_rows[0][None] + shift_x[:, None, None]
    velocity_y = drift_rows[1][1:-1][None] + shift_y[:, None, None]
    flux_x = velocity_x * padded
    centre = padded[:, 1:-1]
    flux_y = velocity_y * centre
    spread = padded[:, 2:] + padded[:, :-2] + column_shift(centre, 1) + column_shift(centre, -1) - 4.0 * centre
    carried = 0.5 * (flux_x[:, 2:] - flux_x[:, :-2]) + 0.5 * (column_shift(flux_y, 1) - column_shift(flux_y, -1))
    return centre + diffusion_rate * spread - carried


def reference(hist, drift, shocks, shock_table, first_weight, mid_weight, head_weight, cotangent):
    density = hist
    drift_pad = jnp.pad(drift, ((0, 0), (1, 1), (0, 0)))
    for section_no in range(STEPS):
        shifts = shock_shift(shocks[:, section_no], shock_table)
        padded = jnp.pad(density, ((0, 0), (1, 1), (0, 0)))
        density = kfe_step(padded, drift_pad, shifts[:, 0], shifts[:, 1])
    inputs = density.astype(jnp.bfloat16).reshape(S, G * G)
    first = jnp.tanh(jnp.dot(inputs, first_weight, preferred_element_type=jnp.float32)).astype(jnp.bfloat16)
    second = jnp.tanh(jnp.dot(first, mid_weight, preferred_element_type=jnp.float32)).astype(jnp.bfloat16)
    second_f = second.astype(jnp.float32)
    value = jnp.dot(second_f, head_weight, precision=lax.Precision.HIGHEST)
    grad_head = jnp.dot(cotangent, second_f, precision=lax.Precision.HIGHEST)
    back_second = (cotangent[:, None] * head_weight[None, :] * (1.0 - second_f * second_f)).astype(jnp.bfloat16)
    grad_mid = jnp.dot(first.T, back_second, preferred_element_type=jnp.float32).astype(jnp.bfloat16)
    back_raw = jnp.dot(back_second, mid_weight.T, preferred_element_type=jnp.float32)
    first_f = first.astype(jnp.float32)
    back_first = (back_raw * (1.0 - first_f * first_f)).astype(jnp.bfloat16)
    grad_first = jnp.dot(inputs.T, back_first, preferred_element_type=jnp.float32).astype(jnp.bfloat16)
    return density, value, grad_first, grad_mid, grad_head
```

```python
import functools
import jax
import jax.numpy as jnp
from jax import lax
from jax.experimental import pallas as pl
from jax.experimental.pallas import tpu as pltpu
from jax.sharding import PartitionSpec as P

diffusion_rate = 0.24
F32, BF16 = jnp.float32, jnp.bfloat16
VMEM = pl.BlockSpec(memory_space=pltpu.VMEM)
SMEM = pl.BlockSpec(memory_space=pltpu.SMEM)
MESH = pl.DeviceIdType.MESH


def remote(src, dst, send, recv, target):
    return pltpu.make_async_remote_copy(
        src_ref=src,
        dst_ref=dst,
        send_sem=send,
        recv_sem=recv,
        device_id={"grid": target},
        device_id_type=MESH,
    )


def halo_kernel(n, rows, lanes, *refs):
    x_refs, refs = refs[:lanes], refs[lanes:]
    drift_ref, lo_ref, hi_ref, dlo_ref, dhi_ref, up, down, send, recv = refs
    me = lax.axis_index("grid")
    count = up.shape[1]
    barrier = pltpu.get_barrier_semaphore()
    has_next, has_prev = me < n - 1, me > 0

    @pl.when(has_next)
    def _():
        pl.semaphore_signal(barrier, inc=1, device_id={"grid": me + 1}, device_id_type=MESH)

    @pl.when(has_prev)
    def _():
        pl.semaphore_signal(barrier, inc=1, device_id={"grid": me - 1}, device_id_type=MESH)

    @pl.when(has_next)
    def _():
        for i in range(2):
            for k in range(lanes):
                edge = x_refs[k][pl.ds(rows - 2 + i, count, stride=rows), :]
                up[i, :, k * 128 : (k + 1) * 128] = edge.astype(BF16)

    @pl.when(has_prev)
    def _():
        for i in range(2):
            for k in range(lanes):
                edge = x_refs[k][pl.ds(i, count, stride=rows), :]
                down[i, :, k * 128 : (k + 1) * 128] = edge.astype(BF16)

    pl.semaphore_wait(barrier, has_next.astype(jnp.int32) + has_prev.astype(jnp.int32))

    def upward():
        return (
            remote(up, lo_ref, send.at[0], recv.at[0], me + 1),
            remote(drift_ref, dlo_ref, send.at[1], recv.at[1], me + 1),
        )

    def downward():
        return (
            remote(down, hi_ref, send.at[2], recv.at[2], me - 1),
            remote(drift_ref, dhi_ref, send.at[3], recv.at[3], me - 1),
        )

    @pl.when(has_next)
    def _():
        for copy in upward():
            copy.start()

    @pl.when(has_prev)
    def _():
        for copy in downward():
            copy.start()

    @pl.when(jnp.logical_not(has_next))
    def _():
        hi_ref[...] = jnp.zeros_like(hi_ref)
        dhi_ref[...] = jnp.zeros_like(dhi_ref)

    @pl.when(jnp.logical_not(has_prev))
    def _():
        lo_ref[...] = jnp.zeros_like(lo_ref)
        dlo_ref[...] = jnp.zeros_like(dlo_ref)

    @pl.when(has_next)
    def _():
        for copy in upward():
            copy.wait_send()
        for copy in downward():
            copy.wait_recv()

    @pl.when(has_prev)
    def _():
        for copy in downward():
            copy.wait_send()
        for copy in upward():
            copy.wait_recv()


def halo(n, rows, x2, drift2):
    count, columns = x2.shape[0] // rows, x2.shape[1]
    edge = jax.ShapeDtypeStruct((2, count, columns), BF16)
    side = jax.ShapeDtypeStruct(drift2.shape, F32)
    lanes = columns // 128
    strips = [
        pl.BlockSpec((x2.shape[0], 128), functools.partial(lambda k, i: (0, k), k))
        for k in range(lanes)
    ]
    return pl.pallas_call(
        functools.partial(halo_kernel, n, rows, lanes),
        grid=(1,),
        out_shape=(edge, edge, side, side),
        in_specs=strips + [VMEM],
        out_specs=(VMEM,) * 4,
        scratch_shapes=[
            pltpu.VMEM(edge.shape, BF16),
            pltpu.VMEM(edge.shape, BF16),
            pltpu.SemaphoreType.DMA((4,)),
            pltpu.SemaphoreType.DMA((4,)),
        ],
        compiler_params=pltpu.CompilerParams(
            collective_id=0, has_side_effects=True, vmem_limit_bytes=48 << 20
        ),
    )(*[x2] * lanes, drift2)


def stencil_kernel(
    n, rows, extended, steps, shocks, table, x_ref, lo_ref, hi_ref, drift_ref, dlo_ref, dhi_ref,
    out_ref, flat_ref, coef, *strips
):
    block = lo_ref.shape[1]
    columns = x_ref.shape[1]
    stored = x_ref.shape[0] // block
    extra = extended - stored
    filler = extended - rows - 4
    lanes = columns // 128
    halo_rows, plain = strips[:lanes], strips[lanes:]
    me = lax.axis_index("grid")
    first_no = pl.program_id(0) * block
    lane = lax.broadcasted_iota(jnp.int32, (1, columns), 1)
    not_first = (lane > 0).astype(F32)
    not_last = (lane < columns - 1).astype(F32)

    @pl.when(pl.program_id(0) == 0)
    def _():
        for part in range(2):
            base = part * rows
            pieces = [drift_ref[pl.ds(base, rows), :], dhi_ref[pl.ds(base, 2), :]]
            if filler > 0:
                pieces.append(jnp.zeros((filler, columns), F32))
            pieces.append(dlo_ref[pl.ds(base + rows - 2, 2), :])
            whole = 0.5 * jnp.concatenate(pieces, axis=0)
            before, after = diffusion_rate - whole, diffusion_rate + whole
            if part == 1:
                before, after = before * not_first, after * not_last
            coef[2 * part] = before
            coef[2 * part + 1] = after
        for strip in halo_rows:
            strip[...] = jnp.zeros_like(strip)

    for k in range(lanes if extra else 0):
        part = slice(k * 128, (k + 1) * 128)
        for i in range(2):
            halo_rows[k][pl.ds(i, block, stride=extra), :] = hi_ref[i, :, part].astype(F32)
            halo_rows[k][pl.ds(extra - 2 + i, block, stride=extra), :] = lo_ref[
                i, :, part
            ].astype(F32)

    row = lax.broadcasted_iota(jnp.int32, (extended, columns), 0)
    outside = ((row >= rows) & (row < rows + 2) & (me == n - 1)) | (
        (row >= extended - 2) & (me == 0)
    )

    def one(s, carry):
        c = x_ref[pl.ds(pl.multiple_of(s * stored, 8), stored), :]
        if extra:
            at = pl.ds(pl.multiple_of(s * extra, 8), extra)
            ends = jnp.concatenate([strip[at, :] for strip in halo_rows], axis=1)
            c = jnp.concatenate([c, ends], axis=0)
        for t in range(steps):
            level = shocks[(first_no + s) * steps + t]
            half_x, half_y = 0.5 * table[2 * level], 0.5 * table[2 * level + 1]
            above = (coef[0] - half_x) * c
            below = (coef[1] + half_x) * c
            left = (coef[2] - half_y * not_first) * c
            right = (coef[3] + half_y * not_last) * c
            c = (
                (1.0 - 4.0 * diffusion_rate) * c
                + (pltpu.roll(above, extended - 1, 0) + pltpu.roll(below, 1, 0))
                + (pltpu.roll(left, columns - 1, 1) + pltpu.roll(right, 1, 1))
            )
            if t < steps - 1:
                c = jnp.where(outside, 0.0, c)
        at = pl.ds(pl.multiple_of(s * stored, 8), stored)
        out_ref[at, :] = c[:stored]
        for k in range(lanes):
            plain[k][at, :] = c[:stored, k * 128 : (k + 1) * 128]
        return carry

    lax.fori_loop(0, block, one, 0, unroll=4)
    for r in range(rows):
        for k in range(lanes):
            at = r * columns + k * 128
            row_now = plain[k][pl.ds(r, block, stride=stored), :]
            flat_ref[:, at : at + 128] = row_now.astype(BF16)


def stencil(n, rows, steps, shocks, table, x2, lo, hi, drift2, dlo, dhi):
    columns = x2.shape[1]
    count = x2.shape[0] // rows
    extended = -(-(rows + 4) // 8) * 8
    stored = rows
    if rows % 8:
        stored = extended
        before, after = [jnp.swapaxes(edge, 0, 1).astype(F32) for edge in (lo, hi)]
        filler = jnp.zeros((count, extended - rows - 4, columns), F32)
        x3 = x2.reshape(count, rows, columns)
        x2 = jnp.concatenate([x3, after, filler, before], axis=1).reshape(-1, columns)
    block = max(b for b in (8, 16, 32) if count % b == 0)
    whole = pl.BlockSpec(drift2.shape, lambda i: (0, 0))
    edge = pl.BlockSpec((2, block, columns), lambda i: (0, i, 0))
    cells = pl.BlockSpec((block * stored, columns), lambda i: (i, 0))
    density, flat = pl.pallas_call(
        functools.partial(stencil_kernel, n, rows, extended, steps),
        grid=(count // block,),
        out_shape=(
            jax.ShapeDtypeStruct(x2.shape, F32),
            jax.ShapeDtypeStruct((count, rows * columns), BF16),
        ),
        in_specs=[SMEM, SMEM, cells, edge, edge, whole, whole, whole],
        out_specs=(cells, pl.BlockSpec((block, rows * columns), lambda i: (i, 0))),
        scratch_shapes=[
            pltpu.VMEM((4, extended, columns), F32),
        ]
        + [pltpu.VMEM((block * max(extended - stored, 8), 128), F32)] * (columns // 128)
        + [pltpu.VMEM((block * stored, 128), F32)] * (columns // 128),
    )(shocks, table, x2, lo, hi, drift2, dlo, dhi)
    return density.reshape(count, stored, columns)[:, :rows], flat


def halvings(rows, columns, count):
    plan = []
    for _ in range(count):
        if columns >= 256:
            columns //= 2
            plan.append((1, rows, columns))
        else:
            rows //= 2
            plan.append((0, rows, columns))
    return plan


def reduce_kernel(n, plan, orders, wide, second_pass, *refs):
    stages = len(plan)
    refs = list(refs)
    x_ref = refs.pop(0)
    if second_pass:
        first_ref, v_ref = refs.pop(0), refs.pop(0)
    out_ref = refs.pop(0)
    if second_pass:
        v_out = refs.pop(0)
    streams = len(orders)
    got = [[refs.pop(0) for _ in range(stages)] for _ in range(streams)]
    acc = [[refs.pop(0) for _ in range(stages - 1)] + [None] for _ in range(streams)]
    narrow = [[None] * wide + [refs.pop(0) for _ in range(wide, stages)] for _ in range(streams)]
    if second_pass:
        v_got, v_acc = refs.pop(0), refs.pop(0)
        v_send, v_recv = refs.pop(0), refs.pop(0)
    send, recv = refs

    me = lax.axis_index("grid")
    bits = [lax.rem(me // (1 << b), 2) for b in range(stages)]
    partner = [me + (1 << b) * (1 - 2 * bits[b]) for b in range(stages)]
    height = x_ref.shape[0] // streams

    barrier = pltpu.get_barrier_semaphore()
    for b in range(stages):
        pl.semaphore_signal(barrier, inc=1, device_id={"grid": partner[b]}, device_id_type=MESH)
    pl.semaphore_wait(barrier, stages)

    place = []
    for t in range(streams):
        row, col = t * height, 0
        spots = []
        for s in range(stages):
            dim, r, c = plan[s]
            bit = bits[orders[t][s]]
            if dim == 1:
                col = pl.multiple_of(col + bit * c, 128)
            else:
                row = pl.multiple_of(row + bit * r, 16)
            spots.append((pl.ds(row, r), pl.ds(col, c)))
        place.append(spots)

    def half(t, s, which):
        dim, r, c = plan[s]
        at_row, at_col = (t * height if s == 0 else 0), 0
        if dim == 1:
            at_col = pl.multiple_of(which * c, 128)
        else:
            at_row = pl.multiple_of(at_row + which * r, 16)
        return (x_ref if s == 0 else acc[t][s - 1]), (pl.ds(at_row, r), pl.ds(at_col, c))

    def scatter(t, s):
        b = orders[t][s]
        ref, spot = half(t, s, 1 - bits[b])
        sem = t * 2 * stages + s
        src = ref.at[spot] if s < wide else narrow[t][s]
        return remote(src, got[t][s], send.at[sem], recv.at[sem], partner[b])

    def begin(t, s):
        if s >= wide:
            ref, spot = half(t, s, 1 - bits[orders[t][s]])
            narrow[t][s][...] = ref[spot].astype(BF16)
        scatter(t, s).start()

    def gather(t, s):
        b = orders[t][s]
        sem = t * 2 * stages + stages + s
        spot = out_ref.at[place[t][s]]
        return remote(spot, spot, send.at[sem], recv.at[sem], partner[b])

    def sum_values(s):
        src = v_ref if s == 0 else v_acc.at[s - 1]
        return remote(src, v_got.at[s], v_send.at[s], v_recv.at[s], partner[s])

    for t in range(streams):
        begin(t, 0)
    if second_pass:
        sum_values(0).start()
    for s in range(stages):
        for t in range(streams):
            scatter(t, s).wait_recv()
            ref, spot = half(t, s, bits[orders[t][s]])
            total = ref[spot] + got[t][s][...].astype(F32)
            if s < stages - 1:
                acc[t][s][...] = total
                begin(t, s + 1)
            else:
                if second_pass:
                    first = first_ref[place[t][s]].astype(F32)
                    total = total * (1.0 - first * first)
                else:
                    total = jnp.tanh(total)
                out_ref[place[t][s]] = total.astype(BF16)
                gather(t, s).start()
        if second_pass:
            sum_values(s).wait_recv()
            mine = v_ref[...] if s == 0 else v_acc[s - 1]
            if s < stages - 1:
                v_acc[s] = mine + v_got[s]
                sum_values(s + 1).start()
            else:
                v_out[...] = mine + v_got[s]
    for s in reversed(range(stages)):
        for t in range(streams):
            gather(t, s).wait_recv()
            if s > 0:
                gather(t, s - 1).start()
    for s in range(stages):
        for t in range(streams):
            scatter(t, s).wait_send()
            gather(t, s).wait_send()
        if second_pass:
            sum_values(s).wait_send()


def reduce_gather(n, x, wide, first=None, v=None):
    stages = n.bit_length() - 1
    assert n == 1 << stages
    streams = 2
    plan = halvings(x.shape[0] // streams, x.shape[1], stages)
    orders = [list(range(stages)), list(range(stages))]
    if stages > 2:
        orders[1][1:3] = [2, 1]
    second_pass = first is not None
    out_shape = [jax.ShapeDtypeStruct(x.shape, BF16)]
    operands = [x]
    if second_pass:
        out_shape.append(jax.ShapeDtypeStruct(v.shape, F32))
        operands += [first, v]
    wide = min(wide, stages)
    scratch = [
        pltpu.VMEM(p[1:], F32 if s < wide else BF16)
        for _ in range(streams)
        for s, p in enumerate(plan)
    ]
    scratch += [pltpu.VMEM(p[1:], F32) for _ in range(streams) for p in plan[:-1]]
    scratch += [pltpu.VMEM(p[1:], BF16) for _ in range(streams) for p in plan[wide:]]
    if second_pass:
        scratch += [pltpu.VMEM((stages,) + v.shape, F32)] * 2
        scratch += [pltpu.SemaphoreType.DMA((stages,))] * 2
    scratch += [pltpu.SemaphoreType.DMA((2 * streams * stages,))] * 2
    return pl.pallas_call(
        functools.partial(reduce_kernel, n, plan, orders, wide, second_pass),
        out_shape=tuple(out_shape),
        in_specs=[VMEM] * len(operands),
        out_specs=(VMEM,) * len(out_shape),
        scratch_shapes=scratch,
        compiler_params=pltpu.CompilerParams(
            collective_id=2 if second_pass else 1,
            has_side_effects=True,
            vmem_limit_bytes=48 << 20,
        ),
    )(*operands)


def local(n, hist, drift, shocks, shock_table, first_weight, mid_weight, head_weight, cotangent):
    scenarios, row_count, columns = hist.shape
    x2 = hist.reshape(scenarios * row_count, columns)
    drift2 = drift.reshape(2 * row_count, columns)
    lo, hi, dlo, dhi = halo(n, row_count, x2, drift2)
    density, inputs = stencil(
        n, row_count, shocks.shape[1], shocks.reshape(-1), shock_table.reshape(-1),
        x2, lo, hi, drift2, dlo, dhi,
    )
    partial_first = jnp.dot(inputs, first_weight, preferred_element_type=F32)
    (first_act,) = reduce_gather(n, partial_first, 2)
    second_pre = jnp.dot(first_act, mid_weight, preferred_element_type=F32)
    second_act = jnp.tanh(second_pre).astype(BF16)
    second_f = second_act.astype(F32)
    head_rows = jnp.broadcast_to(head_weight[None, :], (8, head_weight.shape[0]))
    value_part = lax.dot_general(
        head_rows, second_f, (((1,), (1,)), ((), ())), precision=lax.Precision.HIGHEST
    )
    grad_head = jnp.dot(cotangent, second_f, precision=lax.Precision.HIGHEST)
    back_second = (cotangent[:, None] * head_weight[None, :] * (1.0 - second_f * second_f)).astype(
        BF16
    )
    back_part = lax.dot_general(
        back_second, mid_weight, (((1,), (1,)), ((), ())), preferred_element_type=F32
    )
    back_first, value = reduce_gather(n, back_part, 1, first_act, value_part)
    grad_mid = lax.dot_general(
        first_act, back_second, (((0,), (0,)), ((), ())), preferred_element_type=F32
    )
    grad_first = lax.dot_general(
        inputs, back_first, (((0,), (0,)), ((), ())), preferred_element_type=F32
    )
    return (
        density,
        value[0],
        grad_first.astype(BF16),
        grad_mid.astype(BF16),
        grad_head,
    )


def solution(mesh):
    in_specs = (
        P("groups", "grid", None),
        P(None, "grid", None),
        P("groups", None),
        P("groups", None),
        P(("groups", "grid"), None),
        P("groups", "grid"),
        P(("groups", "grid")),
        P("groups"),
    )
    out_specs = (
        P("groups", "grid", None),
        P("groups"),
        P(("groups", "grid"), None),
        P("groups", "grid"),
        P(("groups", "grid")),
    )
    return jax.shard_map(
        functools.partial(local, mesh.shape["grid"]),
        mesh=mesh,
        in_specs=in_specs,
        out_specs=out_specs,
        check_vma=False,
    )
```

```python
import functools
import jax
import jax.numpy as jnp
from jax import lax
from jax.experimental import pallas as pl
from jax.experimental.pallas import tpu as pltpu
from jax.sharding import PartitionSpec as P

diffusion_rate = 0.24
F32, BF16 = jnp.float32, jnp.bfloat16
VMEM = pl.BlockSpec(memory_space=pltpu.VMEM)
SMEM = pl.BlockSpec(memory_space=pltpu.SMEM)
MESH = pl.DeviceIdType.MESH


def remote(src, dst, send, recv, target):
    return pltpu.make_async_remote_copy(
        src_ref=src,
        dst_ref=dst,
        send_sem=send,
        recv_sem=recv,
        device_id={"grid": target},
        device_id_type=MESH,
    )


def halo_kernel(n, rows, lanes, *refs):
    x_refs, refs = refs[:lanes], refs[lanes:]
    drift_ref, lo_ref, hi_ref, dlo_ref, dhi_ref, up, down, send, recv = refs
    me = lax.axis_index("grid")
    count = up.shape[1]
    barrier = pltpu.get_barrier_semaphore()
    has_next, has_prev = me < n - 1, me > 0

    @pl.when(has_next)
    def _():
        pl.semaphore_signal(barrier, inc=1, device_id={"grid": me + 1}, device_id_type=MESH)

    @pl.when(has_prev)
    def _():
        pl.semaphore_signal(barrier, inc=1, device_id={"grid": me - 1}, device_id_type=MESH)

    @pl.when(has_next)
    def _():
        for i in range(2):
            for k in range(lanes):
                edge = x_refs[k][pl.ds(rows - 2 + i, count, stride=rows), :]
                up[i, :, k * 128 : (k + 1) * 128] = edge.astype(BF16)

    @pl.when(has_prev)
    def _():
        for i in range(2):
            for k in range(lanes):
                edge = x_refs[k][pl.ds(i, count, stride=rows), :]
                down[i, :, k * 128 : (k + 1) * 128] = edge.astype(BF16)

    pl.semaphore_wait(barrier, has_next.astype(jnp.int32) + has_prev.astype(jnp.int32))

    def upward():
        return (
            remote(up, lo_ref, send.at[0], recv.at[0], me + 1),
            remote(drift_ref, dlo_ref, send.at[1], recv.at[1], me + 1),
        )

    def downward():
        return (
            remote(down, hi_ref, send.at[2], recv.at[2], me - 1),
            remote(drift_ref, dhi_ref, send.at[3], recv.at[3], me - 1),
        )

    @pl.when(has_next)
    def _():
        for copy in upward():
            copy.start()

    @pl.when(has_prev)
    def _():
        for copy in downward():
            copy.start()

    @pl.when(jnp.logical_not(has_next))
    def _():
        hi_ref[...] = jnp.zeros_like(hi_ref)
        dhi_ref[...] = jnp.zeros_like(dhi_ref)

    @pl.when(jnp.logical_not(has_prev))
    def _():
        lo_ref[...] = jnp.zeros_like(lo_ref)
        dlo_ref[...] = jnp.zeros_like(dlo_ref)

    @pl.when(has_next)
    def _():
        for copy in upward():
            copy.wait_send()
        for copy in downward():
            copy.wait_recv()

    @pl.when(has_prev)
    def _():
        for copy in downward():
            copy.wait_send()
        for copy in upward():
            copy.wait_recv()


def halo(n, rows, x2, drift2):
    count, columns = x2.shape[0] // rows, x2.shape[1]
    edge = jax.ShapeDtypeStruct((2, count, columns), BF16)
    side = jax.ShapeDtypeStruct(drift2.shape, F32)
    lanes = columns // 128
    strips = [
        pl.BlockSpec((x2.shape[0], 128), functools.partial(lambda k, i: (0, k), k))
        for k in range(lanes)
    ]
    return pl.pallas_call(
        functools.partial(halo_kernel, n, rows, lanes),
        grid=(1,),
        out_shape=(edge, edge, side, side),
        in_specs=strips + [VMEM],
        out_specs=(VMEM,) * 4,
        scratch_shapes=[
            pltpu.VMEM(edge.shape, BF16),
            pltpu.VMEM(edge.shape, BF16),
            pltpu.SemaphoreType.DMA((4,)),
            pltpu.SemaphoreType.DMA((4,)),
        ],
        compiler_params=pltpu.CompilerParams(
            collective_id=0, has_side_effects=True, vmem_limit_bytes=48 << 20
        ),
    )(*[x2] * lanes, drift2)


def stencil_kernel(
    n, rows, extended, steps, block, shocks, table, x_ref, lo_ref, hi_ref, drift_ref, dlo_ref, dhi_ref,
    out_ref, flat_ref, coef, *strips
):
    columns = x_ref.shape[1]
    stored = x_ref.shape[0] // block
    extra = extended - stored
    filler = extended - rows - 4
    lanes = columns // 128
    halo_rows, plain = strips[:lanes], strips[lanes:]
    me = lax.axis_index("grid")
    first_no = pl.program_id(0) * block
    lane = lax.broadcasted_iota(jnp.int32, (1, columns), 1)
    not_first = (lane > 0).astype(F32)
    not_last = (lane < columns - 1).astype(F32)

    @pl.when(pl.program_id(0) == 0)
    def _():
        for part in range(2):
            base = part * rows
            pieces = [drift_ref[pl.ds(base, rows), :], dhi_ref[pl.ds(base, 2), :]]
            if filler > 0:
                pieces.append(jnp.zeros((filler, columns), F32))
            pieces.append(dlo_ref[pl.ds(base + rows - 2, 2), :])
            whole = 0.5 * jnp.concatenate(pieces, axis=0)
            before, after = diffusion_rate - whole, diffusion_rate + whole
            if part == 1:
                before, after = before * not_first, after * not_last
            coef[2 * part] = before
            coef[2 * part + 1] = after
        for strip in halo_rows:
            strip[...] = jnp.zeros_like(strip)

    now = pl.ds(pl.multiple_of(first_no, 8), block)
    for k in range(lanes if extra else 0):
        part = slice(k * 128, (k + 1) * 128)
        for i in range(2):
            halo_rows[k][pl.ds(i, block, stride=extra), :] = hi_ref[i, now, part].astype(F32)
            halo_rows[k][pl.ds(extra - 2 + i, block, stride=extra), :] = lo_ref[
                i, now, part
            ].astype(F32)

    row = lax.broadcasted_iota(jnp.int32, (extended, columns), 0)
    outside = ((row >= rows) & (row < rows + 2) & (me == n - 1)) | (
        (row >= extended - 2) & (me == 0)
    )

    def one(s, carry):
        c = x_ref[pl.ds(pl.multiple_of(s * stored, 8), stored), :]
        if extra:
            at = pl.ds(pl.multiple_of(s * extra, 8), extra)
            ends = jnp.concatenate([strip[at, :] for strip in halo_rows], axis=1)
            c = jnp.concatenate([c, ends], axis=0)
        for t in range(steps):
            level = shocks[t, first_no + s]
            half_x, half_y = 0.5 * table[0, level], 0.5 * table[1, level]
            above = (coef[0] - half_x) * c
            below = (coef[1] + half_x) * c
            left = (coef[2] - half_y * not_first) * c
            right = (coef[3] + half_y * not_last) * c
            c = (
                (1.0 - 4.0 * diffusion_rate) * c
                + (pltpu.roll(above, extended - 1, 0) + pltpu.roll(below, 1, 0))
                + (pltpu.roll(left, columns - 1, 1) + pltpu.roll(right, 1, 1))
            )
            if t < steps - 1:
                c = jnp.where(outside, 0.0, c)
        at = pl.ds(pl.multiple_of(s * stored, 8), stored)
        out_ref[at, :] = c[:stored]
        for k in range(lanes):
            plain[k][at, :] = c[:stored, k * 128 : (k + 1) * 128]
        return carry

    lax.fori_loop(0, block, one, 0, unroll=4)
    for r in range(rows):
        for k in range(lanes):
            at = r * columns + k * 128
            row_now = plain[k][pl.ds(r, block, stride=stored), :]
            flat_ref[:, at : at + 128] = row_now.astype(BF16)


def stencil(n, rows, steps, shocks, table, x2, lo, hi, drift2, dlo, dhi):
    columns = x2.shape[1]
    count = x2.shape[0] // rows
    extended = -(-(rows + 4) // 8) * 8
    stored = rows
    if rows % 8:
        stored = extended
        before, after = [jnp.swapaxes(edge, 0, 1).astype(F32) for edge in (lo, hi)]
        filler = jnp.zeros((count, extended - rows - 4, columns), F32)
        x3 = x2.reshape(count, rows, columns)
        x2 = jnp.concatenate([x3, after, filler, before], axis=1).reshape(-1, columns)
    block = max(b for b in (8, 16, 32) if count % b == 0)
    cells = pl.BlockSpec((block * stored, columns), lambda i: (i, 0))
    density, flat = pl.pallas_call(
        functools.partial(stencil_kernel, n, rows, extended, steps, block),
        grid=(count // block,),
        out_shape=(
            jax.ShapeDtypeStruct(x2.shape, F32),
            jax.ShapeDtypeStruct((count, rows * columns), BF16),
        ),
        in_specs=[SMEM, SMEM, cells] + [VMEM] * 5,
        out_specs=(cells, pl.BlockSpec((block, rows * columns), lambda i: (i, 0))),
        scratch_shapes=[
            pltpu.VMEM((4, extended, columns), F32),
        ]
        + [pltpu.VMEM((block * max(extended - stored, 8), 128), F32)] * (columns // 128)
        + [pltpu.VMEM((block * stored, 128), F32)] * (columns // 128),
    )(shocks, table, x2, lo, hi, drift2, dlo, dhi)
    return density.reshape(count, stored, columns)[:, :rows], flat


def halvings(rows, columns, count):
    plan = []
    for _ in range(count):
        if columns >= 256:
            columns //= 2
            plan.append((1, rows, columns))
        else:
            rows //= 2
            plan.append((0, rows, columns))
    return plan


def reduce_kernel(n, plan, orders, wide, second_pass, *refs):
    stages = len(plan)
    refs = list(refs)
    x_ref = refs.pop(0)
    if second_pass:
        first_ref, v_ref = refs.pop(0), refs.pop(0)
    out_ref = refs.pop(0)
    if second_pass:
        v_out = refs.pop(0)
    streams = len(orders)
    got = [[refs.pop(0) for _ in range(stages)] for _ in range(streams)]
    acc = [[refs.pop(0) for _ in range(stages - 1)] + [None] for _ in range(streams)]
    narrow = [[None if s in wide else refs.pop(0) for s in range(stages)] for _ in range(streams)]
    if second_pass:
        v_got, v_acc = refs.pop(0), refs.pop(0)
        v_send, v_recv = refs.pop(0), refs.pop(0)
    send, recv = refs

    me = lax.axis_index("grid")
    bits = [lax.rem(me // (1 << b), 2) for b in range(stages)]
    partner = [me + (1 << b) * (1 - 2 * bits[b]) for b in range(stages)]
    height = x_ref.shape[0] // streams

    barrier = pltpu.get_barrier_semaphore()
    for b in range(stages):
        pl.semaphore_signal(barrier, inc=1, device_id={"grid": partner[b]}, device_id_type=MESH)
    pl.semaphore_wait(barrier, stages)

    place = []
    for t in range(streams):
        row, col = t * height, 0
        spots = []
        for s in range(stages):
            dim, r, c = plan[s]
            bit = bits[orders[t][s]]
            if dim == 1:
                col = pl.multiple_of(col + bit * c, 128)
            else:
                row = pl.multiple_of(row + bit * r, 8)
            spots.append((pl.ds(row, r), pl.ds(col, c)))
        place.append(spots)

    def half(t, s, which):
        dim, r, c = plan[s]
        at_row, at_col = (t * height if s == 0 else 0), 0
        if dim == 1:
            at_col = pl.multiple_of(which * c, 128)
        else:
            at_row = pl.multiple_of(at_row + which * r, 8)
        return (x_ref if s == 0 else acc[t][s - 1]), (pl.ds(at_row, r), pl.ds(at_col, c))

    def scatter(t, s):
        b = orders[t][s]
        ref, spot = half(t, s, 1 - bits[b])
        sem = t * 2 * stages + s
        src = ref.at[spot] if s in wide else narrow[t][s]
        return remote(src, got[t][s], send.at[sem], recv.at[sem], partner[b])

    def begin(t, s):
        if s not in wide:
            ref, spot = half(t, s, 1 - bits[orders[t][s]])
            narrow[t][s][...] = ref[spot].astype(BF16)
        scatter(t, s).start()

    def gather(t, s):
        b = orders[t][s]
        sem = t * 2 * stages + stages + s
        spot = out_ref.at[place[t][s]]
        return remote(spot, spot, send.at[sem], recv.at[sem], partner[b])

    def sum_values(s):
        src = v_ref if s == 0 else v_acc.at[s - 1]
        return remote(src, v_got.at[s], v_send.at[s], v_recv.at[s], partner[s])

    for t in range(streams):
        begin(t, 0)
    if second_pass:
        sum_values(0).start()
    for s in range(stages):
        for t in range(streams):
            scatter(t, s).wait_recv()
            ref, spot = half(t, s, bits[orders[t][s]])
            total = ref[spot] + got[t][s][...].astype(F32)
            if s < stages - 1:
                acc[t][s][...] = total
                begin(t, s + 1)
            else:
                if second_pass:
                    first = first_ref[place[t][s]].astype(F32)
                    total = total * (1.0 - first * first)
                else:
                    total = jnp.tanh(total)
                out_ref[place[t][s]] = total.astype(BF16)
                gather(t, s).start()
        if second_pass:
            sum_values(s).wait_recv()
            mine = v_ref[...] if s == 0 else v_acc[s - 1]
            if s < stages - 1:
                v_acc[s] = mine + v_got[s]
                sum_values(s + 1).start()
            else:
                v_out[...] = mine + v_got[s]
    for s in reversed(range(stages)):
        for t in range(streams):
            gather(t, s).wait_recv()
            if s > 0:
                gather(t, s - 1).start()
    for s in range(stages):
        for t in range(streams):
            scatter(t, s).wait_send()
            gather(t, s).wait_send()
        if second_pass:
            sum_values(s).wait_send()


def reduce_gather(n, x, wide, first=None, v=None):
    stages = n.bit_length() - 1
    assert n == 1 << stages
    streams = 4
    plan = halvings(x.shape[0] // streams, x.shape[1], stages)
    orders = [list(range(stages)) for _ in range(streams)]
    if stages > 2:
        for order in orders[1::2]:
            order[1:3] = [2, 1]
    second_pass = first is not None
    out_shape = [jax.ShapeDtypeStruct(x.shape, BF16)]
    operands = [x]
    if second_pass:
        out_shape.append(jax.ShapeDtypeStruct(v.shape, F32))
        operands += [first, v]
    scratch = [
        pltpu.VMEM(p[1:], F32 if s in wide else BF16)
        for _ in range(streams)
        for s, p in enumerate(plan)
    ]
    scratch += [pltpu.VMEM(p[1:], F32) for _ in range(streams) for p in plan[:-1]]
    scratch += [
        pltpu.VMEM(p[1:], BF16)
        for _ in range(streams)
        for s, p in enumerate(plan)
        if s not in wide
    ]
    if second_pass:
        scratch += [pltpu.VMEM((stages,) + v.shape, F32)] * 2
        scratch += [pltpu.SemaphoreType.DMA((stages,))] * 2
    scratch += [pltpu.SemaphoreType.DMA((2 * streams * stages,))] * 2
    return pl.pallas_call(
        functools.partial(reduce_kernel, n, plan, orders, wide, second_pass),
        out_shape=tuple(out_shape),
        in_specs=[VMEM] * len(operands),
        out_specs=(VMEM,) * len(out_shape),
        scratch_shapes=scratch,
        compiler_params=pltpu.CompilerParams(
            collective_id=2 if second_pass else 1,
            has_side_effects=True,
            vmem_limit_bytes=48 << 20,
        ),
    )(*operands)


def local(n, hist, drift, shocks, shock_table, first_weight, mid_weight, head_weight, cotangent):
    scenarios, row_count, columns = hist.shape
    x2 = hist.reshape(scenarios * row_count, columns)
    drift2 = drift.reshape(2 * row_count, columns)
    lo, hi, dlo, dhi = halo(n, row_count, x2, drift2)
    density, inputs = stencil(
        n, row_count, shocks.shape[1], shocks.T, shock_table.T,
        x2, lo, hi, drift2, dlo, dhi,
    )
    partial_first = jnp.dot(inputs, first_weight, preferred_element_type=F32)
    (first_act,) = reduce_gather(n, partial_first, (0, 2))
    second_pre = jnp.dot(first_act, mid_weight, preferred_element_type=F32)
    second_act = jnp.tanh(second_pre).astype(BF16)
    second_f = second_act.astype(F32)
    head_rows = jnp.broadcast_to(head_weight[None, :], (8, head_weight.shape[0]))
    value_part = lax.dot_general(
        head_rows, second_f, (((1,), (1,)), ((), ())), precision=lax.Precision.HIGHEST
    )
    grad_head = jnp.dot(cotangent, second_f, precision=lax.Precision.HIGHEST)
    back_second = (cotangent[:, None] * head_weight[None, :] * (1.0 - second_f * second_f)).astype(
        BF16
    )
    back_part = lax.dot_general(
        back_second, mid_weight, (((1,), (1,)), ((), ())), preferred_element_type=F32
    )
    back_first, value = reduce_gather(n, back_part, (0,), first_act, value_part)
    grad_mid = lax.dot_general(
        first_act, back_second, (((0,), (0,)), ((), ())), preferred_element_type=F32
    )
    grad_first = lax.dot_general(
        inputs, back_first, (((0,), (0,)), ((), ())), preferred_element_type=F32
    )
    return (
        density,
        value[0],
        grad_first.astype(BF16),
        grad_mid.astype(BF16),
        grad_head,
    )


def solution(mesh):
    in_specs = (
        P("groups", "grid", None),
        P(None, "grid", None),
        P("groups", None),
        P("groups", None),
        P(("groups", "grid"), None),
        P("groups", "grid"),
        P(("groups", "grid")),
        P("groups"),
    )
    out_specs = (
        P("groups", "grid", None),
        P("groups"),
        P(("groups", "grid"), None),
        P("groups", "grid"),
        P(("groups", "grid")),
    )
    return jax.shard_map(
        functools.partial(local, mesh.shape["grid"]),
        mesh=mesh,
        in_specs=in_specs,
        out_specs=out_specs,
        check_vma=False,
    )
```
